128 devices in a mesh: gx: 8 (over x, core), gy: 16 (over z, y).
Axes of the slice: x: 4, y: 4, z: 4, core: 2. Of those that a mesh axis runs over, the one named last changes fastest.
Arguments:
- velocity: float32 [3, 2, 2048, 2048], P(None, None, 'gx', 'gy'), may hold values from -20 to 20
- viscosity: float32 [2, 2048, 2048], P(None, 'gx', 'gy'), may hold values from 1 to 16
Outputs:
- velocity_new: float32 [3, 2, 2048, 2048], P(None, None, 'gx', 'gy')
The draws below stay inside these ranges and needn't reach their ends.
All inputs are finite; a program needn't handle non-finite values.
Results may differ from the reference program's by a relative error of at most 0.00035.
Values sent between devices are 32-bit elements; how exact they have to be, the bound alone decides.
A program may use at most 64 MiB of HBM per device.

```python
import math
import jax
import jax.numpy as jnp
from jax import lax

NX = 2048
NY = 2048
Z = 2


def profile(key, copies, length):
    keys = jax.random.split(key, 2)
    waves = jax.random.randint(keys[0], (copies, 1), 1, 4).astype(jnp.float32)
    phases = jax.random.uniform(keys[1], (copies, 1), minval=-math.pi, maxval=math.pi)
    position = ((jnp.arange(length, dtype=jnp.float32) + 0.5) / length).reshape(1, length)
    return 0.85 + 0.15 * jnp.sin(2.0 * math.pi * waves * position + phases)


def draw_velocity(key, part):
    keys = jax.random.split(key, 9)
    xcoord = ((jnp.arange(NX, dtype=jnp.float32) + 0.5) / NX).reshape(1, 1, NX, 1)
    ycoord = ((jnp.arange(NY, dtype=jnp.float32) + 0.5) / NY).reshape(1, 1, 1, NY)
    amplitudes = jax.random.uniform(keys[0], (3, 3), minval=-1.0, maxval=1.0)
    modes_x = jax.random.randint(keys[1], (3, 3), 1, 5).astype(jnp.float32)
    modes_y = jax.random.randint(keys[2], (3, 3), 1, 5).astype(jnp.float32)
    planes = jax.random.uniform(keys[3], (3, Z), minval=0.5, maxval=1.5)
    smooth = jnp.zeros((3, 1, NX, NY), jnp.float32)
    for index in range(3):
        weight_here = amplitudes[:, index].reshape(3, 1, 1, 1)
        wave_x = jnp.sin(math.pi * modes_x[:, index].reshape(3, 1, 1, 1) * xcoord)
        wave_y = jnp.sin(math.pi * modes_y[:, index].reshape(3, 1, 1, 1) * ycoord)
        smooth = smooth + weight_here * wave_x * wave_y
    smooth = smooth * planes.reshape(3, Z, 1, 1)
    spread = 6.0
    rough_xcells = jax.random.uniform(keys[4], (3, Z, NX, 1), minval=-spread, maxval=spread)
    rough_xcells = rough_xcells * profile(keys[5], 3 * Z, NY).reshape(3, Z, 1, NY)
    rough_ycells = jax.random.uniform(keys[6], (3, Z, 1, NY), minval=-spread, maxval=spread)
    rough_ycells = rough_ycells * profile(keys[7], 3 * Z, NX).reshape(3, Z, NX, 1)
    rough = 0.25 * jax.random.truncated_normal(keys[8], -4.0, 4.0, (3, Z, NX, NY))
    return (smooth + rough_xcells + rough_ycells + rough).astype(jnp.float32)


def level_of(stream_key, shape, pieces, smallest, top_value):
    def one(dim, parts):
        draws = jax.random.uniform(jax.random.fold_in(jax.random.fold_in(stream_key, 6), dim), (parts,), jnp.float32, smallest / len(pieces), top_value / len(pieces))
        return jnp.repeat(jnp.exp(draws), shape[dim] // parts).reshape((-1,) + (1,) * (len(shape) - dim - 1))

    gain = one(*pieces[0])
    for cut in pieces[1:]:
        gain = gain * one(*cut)
    return gain


def setup_inputs(seed: int = 0) -> dict:
    splits = jax.random.split(jax.random.key(seed), 3)
    velocity = draw_velocity(jax.random.fold_in(splits[2], 71), 0)
    viscosity = jnp.clip(jnp.exp(math.log(16.0) - 2.7725887 * jax.random.uniform(splits[1], (Z, NX, NY), jnp.float32) ** level_of(splits[1], (Z, NX, NY), ((1, 8), (2, 16)), -0.2, 0.2)), 1.0, 16.0)
    return dict(velocity=velocity, viscosity=viscosity)


diffusion = 10000.0


def thomas(coeffs, rights):
    coupling = diffusion * coeffs

    def forward(carry, item):
        prev_c, prev_d = carry
        couple_row, right_row = item
        pivot = 1.0 + 2.0 * couple_row + couple_row * prev_c
        new_c = -couple_row / pivot
        new_d = (right_row + couple_row * prev_d) / pivot
        return (new_c, new_d), (new_c, new_d)

    start = (jnp.zeros_like(coupling[0]), jnp.zeros_like(rights[0]))
    _, (c_all, d_all) = lax.scan(forward, start, (coupling, rights))

    def backward(later, item):
        upper_row, value_row = item
        result = value_row - upper_row * later
        return result, result

    _, solved = lax.scan(backward, jnp.zeros_like(rights[0]), (c_all, d_all), reverse=True)
    return solved


def reference(velocity, viscosity):
    lines = jnp.moveaxis(velocity, 2, 0)
    kappa_x = jnp.moveaxis(viscosity, 1, 0)[:, None]
    xsolved = thomas(kappa_x, lines)
    ylines = xsolved.transpose(3, 1, 2, 0)
    kappa_y = viscosity.transpose(2, 0, 1)[:, None]
    ysolved = thomas(kappa_y, ylines)
    return ysolved.transpose(1, 2, 3, 0)
```

```python
import functools

import jax
import jax.numpy as jnp
from jax import lax
from jax.experimental import pallas as pl
from jax.experimental.pallas import tpu as pltpu
from jax.sharding import PartitionSpec as P

diffusion = 10000.0
MESH = pl.DeviceIdType.MESH
CH = 8
LANES = 128


def row8(ref_or_value):
    return jnp.broadcast_to(ref_or_value, (CH, LANES))


def fundamental(load_eps, phi, psi, ends, cols, steps):
    one = jnp.ones((CH, LANES), jnp.float32)
    zero = jnp.zeros((CH, LANES), jnp.float32)
    state = [(one, zero, zero, one) for _ in range(cols)]
    for t in range(steps):
        for col in range(cols):
            a, da, b, db = state[col]
            phi[col, t] = a
            psi[col, t] = b
            e = load_eps(col, t)
            da = da + e * a
            db = db + e * b
            state[col] = (a + da, da, b + db, db)
    for col in range(cols):
        a, da, b, db = state[col]
        ends[0, col] = a
        ends[1, col] = b
        ends[2, col] = da
        ends[3, col] = db


def chunk_states(ends, states, coef, cols):
    one = jnp.ones((cols, LANES), jnp.float32)
    zero = jnp.zeros((cols, LANES), jnp.float32)
    f, df, m, v = one, zero, zero, one
    n, z = zero, one
    for q in range(CH):
        a, b, da, db = [ends[k, :, q, :] for k in range(4)]
        states[0, :, q, :] = m
        states[1, :, q, :] = v
        f, df = a * f + b * df, da * f + db * df
        m, v = a * m + b * v, da * m + db * v
        r = CH - 1 - q
        a, b, da, db = [ends[k, :, r, :] for k in range(4)]
        n, z = db * n + b * z, a * z + da * n
        states[2, :, r, :] = n
        states[3, :, r, :] = z
    coef[0 * cols : 1 * cols, :] = f
    coef[1 * cols : 2 * cols, :] = m
    coef[2 * cols : 3 * cols, :] = df
    coef[3 * cols : 4 * cols, :] = v
    return m, 1.0 / m


def weights(load_eps, phi, psi, aw, bw, states, whole, inverse, cols, steps):
    for col in range(cols):
        w = row8(whole[col : col + 1, :])
        k = row8(inverse[col : col + 1, :])
        ms, vs, ns, zs = [states[j, col] * k for j in range(4)]
        for t in range(steps):
            a = phi[col, t]
            b = psi[col, t]
            we = load_eps(col, t) * w
            alpha = ns * a - zs * b
            beta = ms * a + vs * b
            phi[col, t] = alpha
            psi[col, t] = beta
            aw[col, t] = alpha * we
            bw[col, t] = beta * we


def totals(load_f, aw, bw, cols, steps, col):
    zero = jnp.zeros((CH, LANES), jnp.float32)
    left = [zero] * 3
    right = [zero] * 3
    for t in range(steps):
        a = aw[col, t]
        b = bw[col, t]
        for c in range(3):
            f = load_f(c, col, t)
            left[c] = left[c] + a * f
            right[c] = right[c] + b * f
    return left, right


def scan_up(x, places):
    for d in (1, 2, 4):
        x = x + jnp.where(places >= d, pltpu.roll(x, d, 0), 0.0)
    return x


def scan_down(x, places):
    for d in (1, 2, 4):
        x = x + jnp.where(places < CH - d, pltpu.roll(x, CH - d, 0), 0.0)
    return x


def interior(load_f, alpha, beta, aw, bw, tots, part, cols, steps):
    places = lax.broadcasted_iota(jnp.int32, (CH, LANES), 0)
    for col in range(cols):
        pre, suf = [], []
        for c in range(3):
            left = tots[0, c, col]
            right = tots[1, c, col]
            pre.append(scan_up(right, places) - right)
            suf.append(scan_down(left, places))
        for t in range(steps):
            a, b = aw[col, t], bw[col, t]
            al, be = alpha[col, t], beta[col, t]
            for c in range(3):
                f = load_f(c, col, t)
                pre[c] = pre[c] + b * f
                suf[c] = suf[c] - a * f
                part[c, col, t] = al * pre[c] + be * suf[c]


def green(coef, nodes, wts, me, devices, rows):
    m = jnp.ones((rows, LANES), jnp.float32)
    v = m
    n = jnp.zeros((rows, LANES), jnp.float32)
    z = jnp.ones((rows, LANES), jnp.float32)
    ms, ns = [m], [n]
    nodes[0, 0] = m
    nodes[1, devices] = n
    for p in range(devices):
        a, b, da, db = [coef[p, k * rows : (k + 1) * rows, :] for k in range(4)]
        m, v = a * m + b * v, da * m + db * v
        ms.append(m)
        nodes[0, p + 1] = m
        r = devices - 1 - p
        a, b, da, db = [coef[r, k * rows : (k + 1) * rows, :] for k in range(4)]
        n, z = db * n + b * z, a * z + da * n
        ns.append(n)
        nodes[1, r] = n
    ns = ns[::-1]
    inverse = 1.0 / m
    for side in range(2):
        at = me + side
        mm = nodes[0, at] * inverse
        nn = nodes[1, at] * inverse
        g = [jnp.where(p <= at, ms[p] * nn, ns[p] * mm) for p in range(devices + 1)]
        for p in range(devices):
            pair = [g[p], g[p + 1]] * (CH // (2 * rows))
            wts[side, p] = jnp.concatenate(pair, axis=0)


def kernel(
    nx, ny, sx, sy,
    visc_hbm, vel_hbm, out_hbm,
    visc, vel, eps, eps_t, out,
    xphi, xpsi, xaw, xbw, xends, xstates, xtots, xpart, xnodes, xwts, xcoef, xsrc,
    yphi, ypsi, yaw, ybw, yends, ystates, ytots, ypart, ynodes, ywts, ycoef, ysrc,
    ut, in_sem, out_sem,
    xc_send, xc_recv, xs_send, xs_recv, yc_send, yc_recv, ys_send, ys_recv,
):
    gx = lax.axis_index("gx")
    gy = lax.axis_index("gy")
    loads = [pltpu.make_async_copy(visc_hbm.at[z], visc.at[z], in_sem.at[z]) for z in range(2)]
    for c in range(3):
        for z in range(2):
            loads.append(
                pltpu.make_async_copy(
                    vel_hbm.at[c, z], vel.at[c, z], in_sem.at[2 + 2 * c + z]
                )
            )
    for copy in loads:
        copy.start()
    barrier = pltpu.get_barrier_semaphore()
    for d in range(1, nx):
        pl.semaphore_signal(
            barrier, inc=1, device_id={"gx": lax.rem(gx + d, nx)}, device_id_type=MESH
        )
    for d in range(1, ny):
        pl.semaphore_signal(
            barrier, inc=1, device_id={"gy": lax.rem(gy + d, ny)}, device_id_type=MESH
        )

    def share(axis, me, devices, buf, send, recv):
        copies = []
        for d in range(1, devices):
            peer = lax.rem(me + d, devices)
            copy = pltpu.make_async_remote_copy(
                src_ref=buf.at[me],
                dst_ref=buf.at[me],
                send_sem=send.at[d - 1],
                recv_sem=recv.at[me],
                device_id={axis: peer},
                device_id_type=MESH,
            )
            copy.start()
            copies.append(copy)
        return copies

    def arrive(axis, me, devices, buf, send, recv):
        for d in range(1, devices):
            peer = lax.rem(me + d, devices)
            pltpu.make_async_remote_copy(
                src_ref=buf.at[peer],
                dst_ref=buf.at[peer],
                send_sem=send.at[d - 1],
                recv_sem=recv.at[peer],
                device_id={axis: peer},
                device_id_type=MESH,
            ).wait_recv()

    for copy in loads[:2]:
        copy.wait()
    for z in range(2):
        eps[z] = 1.0 / (diffusion * visc[z])

    def eps_x(col, t):
        return eps[col, pl.ds(t, CH, stride=sx), :]

    def vel_x(c, col, t):
        return vel[c, col, pl.ds(t, CH, stride=sx), :]

    def eps_y(col, t):
        return eps_t[col, pl.ds(t, CH, stride=sy), :]

    def vel_y(c, col, t):
        return ut[c, col, pl.ds(t, CH, stride=sy), :]

    fundamental(eps_x, xphi, xpsi, xends, 2, sx)
    xwhole, xinv = chunk_states(xends, xstates, xcoef.at[gx], 2)
    pl.semaphore_wait(barrier, nx + ny - 2)
    sent = share("gx", gx, nx, xcoef, xc_send, xc_recv)
    weights(eps_x, xphi, xpsi, xaw, xbw, xstates, xwhole, xinv, 2, sx)
    for copy in loads[2:]:
        copy.wait()
    for col in range(2):
        left, right = totals(vel_x, xaw, xbw, 2, sx, col)
        k = xinv[col : col + 1, :]
        for c in range(3):
            xtots[0, c, col] = left[c]
            xtots[1, c, col] = right[c]
            for lr, value in enumerate((left[c], right[c])):
                at = (c % 2) * 4 + lr * 2 + col
                row = k * jnp.sum(value, axis=0, keepdims=True)
                xsrc[gx, c // 2, at : at + 1, :] = row
    xsrc[gx, 1, 4:8, :] = jnp.zeros((4, LANES), jnp.float32)
    sent += share("gx", gx, nx, xsrc, xs_send, xs_recv)

    for z in range(2):
        for tile in range(2):
            eps_t[2 * z + tile] = eps[z, tile * LANES : (tile + 1) * LANES, :].T
    fundamental(eps_y, yphi, ypsi, yends, 4, sy)
    ywhole, yinv = chunk_states(yends, ystates, ycoef.at[gy], 4)
    sent += share("gy", gy, ny, ycoef, yc_send, yc_recv)
    interior(vel_x, xphi, xpsi, xaw, xbw, xtots, xpart, 2, sx)
    weights(eps_y, yphi, ypsi, yaw, ybw, ystates, ywhole, yinv, 4, sy)
    arrive("gx", gx, nx, xcoef, xc_send, xc_recv)
    green(xcoef, xnodes, xwts, gx, nx, 2)

    arrive("gx", gx, nx, xsrc, xs_send, xs_recv)
    ends = []
    for side in range(2):
        tiles = []
        for k in range(2):
            acc = xwts[side, 0] * xsrc[0, k]
            for p in range(1, nx):
                acc = acc + xwts[side, p] * xsrc[p, k]
            tiles.append(acc + pltpu.roll(acc, CH - 2, 0))
        ends.append(tiles)
    for col in range(2):
        for c in range(3):
            at = (c % 2) * 4 + col
            s = row8(ends[0][c // 2][at : at + 1, :])
            r = row8(ends[1][c // 2][at : at + 1, :])
            for t in range(sx):
                vel[c, col, pl.ds(t, CH, stride=sx), :] = (
                    xpart[c, col, t] + xphi[col, t] * s + xpsi[col, t] * r
                )

    for col in range(4):
        z, tile = col // 2, col % 2
        for c in range(3):
            ut[c, col] = vel[c, z, tile * LANES : (tile + 1) * LANES, :].T
        left, right = totals(vel_y, yaw, ybw, 4, sy, col)
        k = yinv[col : col + 1, :]
        for c in range(3):
            ytots[0, c, col] = left[c]
            ytots[1, c, col] = right[c]
            for lr, value in enumerate((left[c], right[c])):
                at = lr * 4 + col
                ysrc[gy, c, at : at + 1, :] = k * jnp.sum(value, axis=0, keepdims=True)
    sent += share("gy", gy, ny, ysrc, ys_send, ys_recv)
    arrive("gy", gy, ny, ycoef, yc_send, yc_recv)
    green(ycoef, ynodes, ywts, gy, ny, 4)
    interior(vel_y, yphi, ypsi, yaw, ybw, ytots, ypart, 4, sy)

    arrive("gy", gy, ny, ysrc, ys_send, ys_recv)
    ends = []
    for side in range(2):
        tiles = []
        for c in range(3):
            acc = ywts[side, 0] * ysrc[0, c]
            for p in range(1, ny):
                acc = acc + ywts[side, p] * ysrc[p, c]
            tiles.append(acc + pltpu.roll(acc, 4, 0))
        ends.append(tiles)
    stores = []
    for c in range(3):
        for z in range(2):
            for tile in range(2):
                col = 2 * z + tile
                s = row8(ends[0][c][col : col + 1, :])
                r = row8(ends[1][c][col : col + 1, :])
                for t in range(sy):
                    ut[c, col, pl.ds(t, CH, stride=sy), :] = (
                        ypart[c, col, t] + yphi[col, t] * s + ypsi[col, t] * r
                    )
                out[c, z, tile * LANES : (tile + 1) * LANES, :] = ut[c, col].T
            store = pltpu.make_async_copy(out.at[c, z], out_hbm.at[c, z], out_sem.at[2 * c + z])
            store.start()
            stores.append(store)
    for copy in sent:
        copy.wait_send()
    for store in stores:
        store.wait()


def on_device(nx, ny, velocity, viscosity):
    lx, ly = velocity.shape[2], velocity.shape[3]
    sx, sy = lx // CH, ly // CH
    f32 = jnp.float32
    vm = lambda *shape: pltpu.VMEM(shape, f32)
    dma = lambda n: pltpu.SemaphoreType.DMA((n,))

    def phase(cols, steps, devices, rows, coefs, srcs):
        return [
            vm(cols, steps, CH, LANES),
            vm(cols, steps, CH, LANES),
            vm(cols, steps, CH, LANES),
            vm(cols, steps, CH, LANES),
            vm(4, cols, CH, LANES),
            vm(4, cols, CH, LANES),
            vm(2, 3, cols, CH, LANES),
            vm(3, cols, steps, CH, LANES),
            vm(2, devices + 1, rows, LANES),
            vm(2, devices, CH, LANES),
            vm(devices, coefs, LANES),
            vm(devices, srcs, CH, LANES),
        ]

    return pl.pallas_call(
        functools.partial(kernel, nx, ny, sx, sy),
        out_shape=jax.ShapeDtypeStruct(velocity.shape, f32),
        in_specs=[pl.BlockSpec(memory_space=pl.ANY)] * 2,
        out_specs=pl.BlockSpec(memory_space=pl.ANY),
        scratch_shapes=[
            vm(2, lx, ly),
            vm(3, 2, lx, ly),
            vm(2, lx, ly),
            vm(4, ly, LANES),
            vm(3, 2, lx, ly),
            *phase(2, sx, nx, 2, 8, 2),
            *phase(4, sy, ny, 4, 16, 3),
            vm(3, 4, ly, LANES),
            dma(8),
            dma(6),
            dma(nx), dma(nx), dma(nx), dma(nx),
            dma(ny), dma(ny), dma(ny), dma(ny),
        ],
        compiler_params=pltpu.CompilerParams(collective_id=0, has_side_effects=True),
    )(viscosity, velocity)


def solution(mesh):
    return jax.shard_map(
        functools.partial(on_device, mesh.shape["gx"], mesh.shape["gy"]),
        mesh=mesh,
        in_specs=(P(None, None, "gx", "gy"), P(None, "gx", "gy")),
        out_specs=P(None, None, "gx", "gy"),
        check_vma=False,
    )
```

```python
import functools

import jax
import jax.numpy as jnp
from jax import lax
from jax.experimental import pallas as pl
from jax.experimental.pallas import tpu as pltpu
from jax.sharding import PartitionSpec as P

diffusion = 10000.0
MESH = pl.DeviceIdType.MESH
CH = 8
LANES = 128


def row8(ref_or_value):
    return jnp.broadcast_to(ref_or_value, (CH, LANES))


def fundamental(load_eps, phi, psi, ends, cols, steps):
    one = jnp.ones((CH, LANES), jnp.float32)
    zero = jnp.zeros((CH, LANES), jnp.float32)
    state = [(one, zero, zero, one) for _ in range(cols)]
    for t in range(steps):
        for col in range(cols):
            a, da, b, db = state[col]
            phi[col, t] = a
            psi[col, t] = b
            e = load_eps(col, t)
            da = da + e * a
            db = db + e * b
            state[col] = (a + da, da, b + db, db)
    for col in range(cols):
        a, da, b, db = state[col]
        ends[0, col] = a
        ends[1, col] = b
        ends[2, col] = da
        ends[3, col] = db


def chunk_states(ends, states, coef, cols):
    one = jnp.ones((cols, LANES), jnp.float32)
    zero = jnp.zeros((cols, LANES), jnp.float32)
    f, df, m, v = one, zero, zero, one
    n, z = zero, one
    for q in range(CH):
        a, b, da, db = [ends[k, :, q, :] for k in range(4)]
        states[0, :, q, :] = m
        states[1, :, q, :] = v
        f, df = a * f + b * df, da * f + db * df
        m, v = a * m + b * v, da * m + db * v
        r = CH - 1 - q
        a, b, da, db = [ends[k, :, r, :] for k in range(4)]
        n, z = db * n + b * z, a * z + da * n
        states[2, :, r, :] = n
        states[3, :, r, :] = z
    coef[0 * cols : 1 * cols, :] = f
    coef[1 * cols : 2 * cols, :] = m
    coef[2 * cols : 3 * cols, :] = df
    coef[3 * cols : 4 * cols, :] = v
    return m, 1.0 / m


def weights(load_eps, phi, psi, aw, bw, states, whole, inverse, cols, steps):
    for col in range(cols):
        w = row8(whole[col : col + 1, :])
        k = row8(inverse[col : col + 1, :])
        ms, vs, ns, zs = [states[j, col] * k for j in range(4)]
        for t in range(steps):
            a = phi[col, t]
            b = psi[col, t]
            we = load_eps(col, t) * w
            alpha = ns * a - zs * b
            beta = ms * a + vs * b
            phi[col, t] = alpha
            psi[col, t] = beta
            aw[col, t] = alpha * we
            bw[col, t] = beta * we


def totals(load_f, aw, bw, cols, steps, col):
    zero = jnp.zeros((CH, LANES), jnp.float32)
    left = [zero] * 3
    right = [zero] * 3
    for t in range(steps):
        a = aw[col, t]
        b = bw[col, t]
        for c in range(3):
            f = load_f(c, col, t)
            left[c] = left[c] + a * f
            right[c] = right[c] + b * f
    return left, right


def scan_up(x, places):
    for d in (1, 2, 4):
        x = x + jnp.where(places >= d, pltpu.roll(x, d, 0), 0.0)
    return x


def scan_down(x, places):
    for d in (1, 2, 4):
        x = x + jnp.where(places < CH - d, pltpu.roll(x, CH - d, 0), 0.0)
    return x


def interior(load_f, alpha, beta, aw, bw, tots, part, cols, steps):
    places = lax.broadcasted_iota(jnp.int32, (CH, LANES), 0)
    for col in range(cols):
        pre, suf = [], []
        for c in range(3):
            left = tots[0, c, col]
            right = tots[1, c, col]
            pre.append(scan_up(right, places) - right)
            suf.append(scan_down(left, places))
        for t in range(steps):
            a, b = aw[col, t], bw[col, t]
            al, be = alpha[col, t], beta[col, t]
            for c in range(3):
                f = load_f(c, col, t)
                pre[c] = pre[c] + b * f
                suf[c] = suf[c] - a * f
                part[c, col, t] = al * pre[c] + be * suf[c]


def green(coef, nodes, wts, me, devices, rows):
    m = jnp.ones((rows, LANES), jnp.float32)
    v = m
    n = jnp.zeros((rows, LANES), jnp.float32)
    z = jnp.ones((rows, LANES), jnp.float32)
    ms, ns = [m], [n]
    nodes[0, 0] = m
    nodes[1, devices] = n
    for p in range(devices):
        a, b, da, db = [coef[p, k * rows : (k + 1) * rows, :] for k in range(4)]
        m, v = a * m + b * v, da * m + db * v
        ms.append(m)
        nodes[0, p + 1] = m
        r = devices - 1 - p
        a, b, da, db = [coef[r, k * rows : (k + 1) * rows, :] for k in range(4)]
        n, z = db * n + b * z, a * z + da * n
        ns.append(n)
        nodes[1, r] = n
    ns = ns[::-1]
    inverse = 1.0 / m
    for side in range(2):
        at = me + side
        mm = nodes[0, at] * inverse
        nn = nodes[1, at] * inverse
        g = [jnp.where(p <= at, ms[p] * nn, ns[p] * mm) for p in range(devices + 1)]
        for p in range(devices):
            pair = [g[p], g[p + 1]] * (CH // (2 * rows))
            wts[side, p] = jnp.concatenate(pair, axis=0)


def kernel(
    nx, ny, sx, sy,
    visc_hbm, vel_hbm, ypart, yphi, ypsi, yends_out,
    visc, vel, eps, eps_t,
    xphi, xpsi, xaw, xbw, xends, xstates, xtots, xpart, xnodes, xwts, xcoef, xsrc,
    yaw, ybw, yends, ystates, ytots, ynodes, ywts, ycoef, ysrc,
    ut, in_sem,
    xc_send, xc_recv, xs_send, xs_recv, yc_send, yc_recv, ys_send, ys_recv,
):
    gx = lax.axis_index("gx")
    gy = lax.axis_index("gy")
    loads = [pltpu.make_async_copy(visc_hbm.at[z], visc.at[z], in_sem.at[z]) for z in range(2)]
    for c in range(3):
        for z in range(2):
            loads.append(
                pltpu.make_async_copy(
                    vel_hbm.at[c, z], vel.at[c, z], in_sem.at[2 + 2 * c + z]
                )
            )
    for copy in loads:
        copy.start()
    barrier = pltpu.get_barrier_semaphore()
    for d in range(1, nx):
        pl.semaphore_signal(
            barrier, inc=1, device_id={"gx": lax.rem(gx + d, nx)}, device_id_type=MESH
        )
    for d in range(1, ny):
        pl.semaphore_signal(
            barrier, inc=1, device_id={"gy": lax.rem(gy + d, ny)}, device_id_type=MESH
        )

    def share(axis, me, devices, buf, send, recv):
        copies = []
        for d in range(1, devices):
            peer = lax.rem(me + d, devices)
            copy = pltpu.make_async_remote_copy(
                src_ref=buf.at[me],
                dst_ref=buf.at[me],
                send_sem=send.at[d - 1],
                recv_sem=recv.at[me],
                device_id={axis: peer},
                device_id_type=MESH,
            )
            copy.start()
            copies.append(copy)
        return copies

    def arrive(axis, me, devices, buf, send, recv):
        for d in range(1, devices):
            peer = lax.rem(me + d, devices)
            pltpu.make_async_remote_copy(
                src_ref=buf.at[peer],
                dst_ref=buf.at[peer],
                send_sem=send.at[d - 1],
                recv_sem=recv.at[peer],
                device_id={axis: peer},
                device_id_type=MESH,
            ).wait_recv()

    for copy in loads[:2]:
        copy.wait()
    for z in range(2):
        eps[z] = 1.0 / (diffusion * visc[z])

    def eps_x(col, t):
        return eps[col, pl.ds(t, CH, stride=sx), :]

    def vel_x(c, col, t):
        return vel[c, col, pl.ds(t, CH, stride=sx), :]

    def eps_y(col, t):
        return eps_t[col, pl.ds(t, CH, stride=sy), :]

    def vel_y(c, col, t):
        return ut[c, col, pl.ds(t, CH, stride=sy), :]

    fundamental(eps_x, xphi, xpsi, xends, 2, sx)
    xwhole, xinv = chunk_states(xends, xstates, xcoef.at[gx], 2)
    pl.semaphore_wait(barrier, nx + ny - 2)
    sent = share("gx", gx, nx, xcoef, xc_send, xc_recv)
    weights(eps_x, xphi, xpsi, xaw, xbw, xstates, xwhole, xinv, 2, sx)
    for copy in loads[2:]:
        copy.wait()
    for col in range(2):
        left, right = totals(vel_x, xaw, xbw, 2, sx, col)
        k = xinv[col : col + 1, :]
        for c in range(3):
            xtots[0, c, col] = left[c]
            xtots[1, c, col] = right[c]
            for lr, value in enumerate((left[c], right[c])):
                at = (c % 2) * 4 + lr * 2 + col
                row = k * jnp.sum(value, axis=0, keepdims=True)
                xsrc[gx, c // 2, at : at + 1, :] = row
    xsrc[gx, 1, 4:8, :] = jnp.zeros((4, LANES), jnp.float32)
    sent += share("gx", gx, nx, xsrc, xs_send, xs_recv)

    for z in range(2):
        for tile in range(2):
            eps_t[2 * z + tile] = eps[z, tile * LANES : (tile + 1) * LANES, :].T
    fundamental(eps_y, yphi, ypsi, yends, 4, sy)
    ywhole, yinv = chunk_states(yends, ystates, ycoef.at[gy], 4)
    sent += share("gy", gy, ny, ycoef, yc_send, yc_recv)
    interior(vel_x, xphi, xpsi, xaw, xbw, xtots, xpart, 2, sx)
    weights(eps_y, yphi, ypsi, yaw, ybw, ystates, ywhole, yinv, 4, sy)
    arrive("gx", gx, nx, xcoef, xc_send, xc_recv)
    green(xcoef, xnodes, xwts, gx, nx, 2)

    arrive("gx", gx, nx, xsrc, xs_send, xs_recv)
    ends = []
    for side in range(2):
        tiles = []
        for k in range(2):
            acc = xwts[side, 0] * xsrc[0, k]
            for p in range(1, nx):
                acc = acc + xwts[side, p] * xsrc[p, k]
            tiles.append(acc + pltpu.roll(acc, CH - 2, 0))
        ends.append(tiles)
    for col in range(2):
        for c in range(3):
            at = (c % 2) * 4 + col
            s = row8(ends[0][c // 2][at : at + 1, :])
            r = row8(ends[1][c // 2][at : at + 1, :])
            for t in range(sx):
                vel[c, col, pl.ds(t, CH, stride=sx), :] = (
                    xpart[c, col, t] + xphi[col, t] * s + xpsi[col, t] * r
                )

    for col in range(4):
        z, tile = col // 2, col % 2
        for c in range(3):
            ut[c, col] = vel[c, z, tile * LANES : (tile + 1) * LANES, :].T
        left, right = totals(vel_y, yaw, ybw, 4, sy, col)
        k = yinv[col : col + 1, :]
        for c in range(3):
            ytots[0, c, col] = left[c]
            ytots[1, c, col] = right[c]
            for lr, value in enumerate((left[c], right[c])):
                at = lr * 4 + col
                ysrc[gy, c, at : at + 1, :] = k * jnp.sum(value, axis=0, keepdims=True)
    sent += share("gy", gy, ny, ysrc, ys_send, ys_recv)
    arrive("gy", gy, ny, ycoef, yc_send, yc_recv)
    green(ycoef, ynodes, ywts, gy, ny, 4)
    interior(vel_y, yphi, ypsi, yaw, ybw, ytots, ypart, 4, sy)

    arrive("gy", gy, ny, ysrc, ys_send, ys_recv)
    for side in range(2):
        for c in range(3):
            acc = ywts[side, 0] * ysrc[0, c]
            for p in range(1, ny):
                acc = acc + ywts[side, p] * ysrc[p, c]
            yends_out[side, c] = acc + pltpu.roll(acc, 4, 0)
    for copy in sent:
        copy.wait_send()


def finish(sy, ypart, yphi, ypsi, ends, out_hbm, turned, out, sem):
    stores = []
    for c in range(3):
        for z in range(2):
            for tile in range(2):
                col = 2 * z + tile
                s = row8(ends[0, c, col : col + 1, :])
                r = row8(ends[1, c, col : col + 1, :])
                for t in range(sy):
                    turned[c, col, pl.ds(t, CH, stride=sy), :] = (
                        ypart[c, col, t] + yphi[col, t] * s + ypsi[col, t] * r
                    )
                out[c, z, tile * LANES : (tile + 1) * LANES, :] = turned[c, col].T
            store = pltpu.make_async_copy(out.at[c, z], out_hbm.at[c, z], sem.at[2 * c + z])
            store.start()
            stores.append(store)
    for store in stores:
        store.wait()


def on_device(nx, ny, velocity, viscosity):
    lx, ly = velocity.shape[2], velocity.shape[3]
    sx, sy = lx // CH, ly // CH
    f32 = jnp.float32
    vm = lambda *shape: pltpu.VMEM(shape, f32)
    dma = lambda n: pltpu.SemaphoreType.DMA((n,))

    def phase(cols, steps, devices, rows, coefs, srcs):
        return [
            vm(cols, steps, CH, LANES),
            vm(cols, steps, CH, LANES),
            vm(4, cols, CH, LANES),
            vm(4, cols, CH, LANES),
            vm(2, 3, cols, CH, LANES),
            vm(2, devices + 1, rows, LANES),
            vm(2, devices, CH, LANES),
            vm(devices, coefs, LANES),
            vm(devices, srcs, CH, LANES),
        ]

    on_chip = pl.BlockSpec(memory_space=pltpu.VMEM)
    in_hbm = pl.BlockSpec(memory_space=pltpu.HBM)
    shape = lambda *dims: jax.ShapeDtypeStruct(dims, f32)
    xphase = phase(2, sx, nx, 2, 8, 2)
    kept = pl.pallas_call(
        functools.partial(kernel, nx, ny, sx, sy),
        out_shape=(
            shape(3, 4, sy, CH, LANES),
            shape(4, sy, CH, LANES),
            shape(4, sy, CH, LANES),
            shape(2, 3, CH, LANES),
        ),
        in_specs=[in_hbm] * 2,
        out_specs=(on_chip,) * 4,
        scratch_shapes=[
            vm(2, lx, ly),
            vm(3, 2, lx, ly),
            vm(2, lx, ly),
            vm(4, ly, LANES),
            vm(2, sx, CH, LANES),
            vm(2, sx, CH, LANES),
            *xphase[:5],
            vm(3, 2, sx, CH, LANES),
            *xphase[5:],
            *phase(4, sy, ny, 4, 16, 3),
            vm(3, 4, ly, LANES),
            dma(8),
            dma(nx), dma(nx), dma(nx), dma(nx),
            dma(ny), dma(ny), dma(ny), dma(ny),
        ],
        compiler_params=pltpu.CompilerParams(
            collective_id=0, has_side_effects=True, vmem_limit_bytes=24 * 2**20
        ),
    )(
        pltpu.with_memory_space_constraint(viscosity, pltpu.HBM),
        pltpu.with_memory_space_constraint(velocity, pltpu.HBM),
    )
    return pl.pallas_call(
        functools.partial(finish, sy),
        out_shape=shape(*velocity.shape),
        in_specs=[on_chip] * 4,
        out_specs=in_hbm,
        scratch_shapes=[
            vm(3, 4, ly, LANES),
            vm(3, 2, lx, ly),
            dma(6),
        ],
        compiler_params=pltpu.CompilerParams(vmem_limit_bytes=16 * 2**20),
    )(*kept)


def solution(mesh):
    return jax.shard_map(
        functools.partial(on_device, mesh.shape["gx"], mesh.shape["gy"]),
        mesh=mesh,
        in_specs=(P(None, None, "gx", "gy"), P(None, "gx", "gy")),
        out_specs=P(None, None, "gx", "gy"),
        check_vma=False,
    )
```

```python
import functools

import jax
import jax.numpy as jnp
from jax import lax
from jax.experimental import pallas as pl
from jax.experimental.pallas import tpu as pltpu
from jax.sharding import PartitionSpec as P

diffusion = 10000.0
MESH = pl.DeviceIdType.MESH
CH = 8
LANES = 128


NEAR = 4


def ring_peers(me, devices, inner):
    outer = devices // inner
    mine_out, mine_in = me // inner, lax.rem(me, inner)
    far = lambda step, size: min(step, size - step) if size > 2 else 0
    steps = [(a, b) for a in range(outer) for b in range(inner) if a or b]
    steps.sort(key=lambda ab: -(far(ab[0], outer) + far(ab[1], inner)))
    return [
        (a, b, lax.rem(mine_out + a, outer) * inner + lax.rem(mine_in + b, inner))
        for a, b in steps
    ]


def row8(ref_or_value):
    return jnp.broadcast_to(ref_or_value, (CH, LANES))


def fundamental(load_eps, phi, psi, ends, cols, steps):
    one = jnp.ones((CH, LANES), jnp.float32)
    zero = jnp.zeros((CH, LANES), jnp.float32)
    state = [(one, zero, zero, one) for _ in range(cols)]
    for t in range(steps):
        for col in range(cols):
            a, da, b, db = state[col]
            phi[col, t] = a
            psi[col, t] = b
            e = load_eps(col, t)
            da = da + e * a
            db = db + e * b
            state[col] = (a + da, da, b + db, db)
    for col in range(cols):
        a, da, b, db = state[col]
        ends[0, col] = a
        ends[1, col] = b
        ends[2, col] = da
        ends[3, col] = db


def chunk_states(ends, states, coef, cols):
    one = jnp.ones((cols, LANES), jnp.float32)
    zero = jnp.zeros((cols, LANES), jnp.float32)
    f, df, m, v = one, zero, zero, one
    n, z = zero, one
    for q in range(CH):
        a, b, da, db = [ends[k, :, q, :] for k in range(4)]
        states[0, :, q, :] = m
        states[1, :, q, :] = v
        f, df = a * f + b * df, da * f + db * df
        m, v = a * m + b * v, da * m + db * v
        r = CH - 1 - q
        a, b, da, db = [ends[k, :, r, :] for k in range(4)]
        n, z = db * n + b * z, a * z + da * n
        states[2, :, r, :] = n
        states[3, :, r, :] = z
    coef[0 * cols : 1 * cols, :] = f
    coef[1 * cols : 2 * cols, :] = m
    coef[2 * cols : 3 * cols, :] = df
    coef[3 * cols : 4 * cols, :] = v
    return m, 1.0 / m


def weights(load_eps, phi, psi, aw, bw, states, whole, inverse, cols, steps):
    for col in range(cols):
        w = row8(whole[col : col + 1, :])
        k = row8(inverse[col : col + 1, :])
        ms, vs, ns, zs = [states[j, col] * k for j in range(4)]
        for t in range(steps):
            a = phi[col, t]
            b = psi[col, t]
            we = load_eps(col, t) * w
            alpha = ns * a - zs * b
            beta = ms * a + vs * b
            phi[col, t] = alpha
            psi[col, t] = beta
            aw[col, t] = alpha * we
            bw[col, t] = beta * we


def totals(load_f, aw, bw, cols, steps, col):
    zero = jnp.zeros((CH, LANES), jnp.float32)
    left = [zero] * 3
    right = [zero] * 3
    for t in range(steps):
        a = aw[col, t]
        b = bw[col, t]
        for c in range(3):
            f = load_f(c, col, t)
            left[c] = left[c] + a * f
            right[c] = right[c] + b * f
    return left, right


def scan_up(x, places):
    for d in (1, 2, 4):
        x = x + jnp.where(places >= d, pltpu.roll(x, d, 0), 0.0)
    return x


def scan_down(x, places):
    for d in (1, 2, 4):
        x = x + jnp.where(places < CH - d, pltpu.roll(x, CH - d, 0), 0.0)
    return x


def interior(load_f, alpha, beta, aw, bw, tots, part, cols, steps):
    places = lax.broadcasted_iota(jnp.int32, (CH, LANES), 0)
    for col in range(cols):
        pre, suf = [], []
        for c in range(3):
            left = tots[0, c, col]
            right = tots[1, c, col]
            pre.append(scan_up(right, places) - right)
            suf.append(scan_down(left, places))
        for t in range(steps):
            a, b = aw[col, t], bw[col, t]
            al, be = alpha[col, t], beta[col, t]
            for c in range(3):
                f = load_f(c, col, t)
                pre[c] = pre[c] + b * f
                suf[c] = suf[c] - a * f
                part[c, col, t] = al * pre[c] + be * suf[c]


def green(coef, nodes, wts, me, devices, rows):
    m = jnp.ones((rows, LANES), jnp.float32)
    v = m
    n = jnp.zeros((rows, LANES), jnp.float32)
    z = jnp.ones((rows, LANES), jnp.float32)
    ms, ns = [m], [n]
    nodes[0, 0] = m
    nodes[1, devices] = n
    for p in range(devices):
        a, b, da, db = [coef[p, k * rows : (k + 1) * rows, :] for k in range(4)]
        m, v = a * m + b * v, da * m + db * v
        ms.append(m)
        nodes[0, p + 1] = m
        r = devices - 1 - p
        a, b, da, db = [coef[r, k * rows : (k + 1) * rows, :] for k in range(4)]
        n, z = db * n + b * z, a * z + da * n
        ns.append(n)
        nodes[1, r] = n
    ns = ns[::-1]
    inverse = 1.0 / m
    for side in range(2):
        at = me + side
        mm = nodes[0, at] * inverse
        nn = nodes[1, at] * inverse
        g = [jnp.where(p <= at, ms[p] * nn, ns[p] * mm) for p in range(devices + 1)]
        for p in range(devices):
            pair = [g[p], g[p + 1]] * (CH // (2 * rows))
            wts[side, p] = jnp.concatenate(pair, axis=0)


def kernel(
    nx, ny, sx, sy,
    visc_hbm, vel_hbm, ypart, yphi, ypsi, yends_out,
    visc, vel, eps, eps_t,
    xphi, xpsi, xaw, xbw, xends, xstates, xtots, xpart, xnodes, xwts, xcoef, xsrc,
    yaw, ybw, yends, ystates, ytots, ynodes, ywts, ycoef, ysrc,
    ut, in_sem, entered,
    xc_send, xc_recv, xs_send, xs_recv, yc_send, yc_recv, ys_send, ys_recv,
):
    gx = lax.axis_index("gx")
    gy = lax.axis_index("gy")
    loads = [pltpu.make_async_copy(visc_hbm.at[z], visc.at[z], in_sem.at[z]) for z in range(2)]
    for c in range(3):
        for z in range(2):
            loads.append(
                pltpu.make_async_copy(
                    vel_hbm.at[c, z], vel.at[c, z], in_sem.at[2 + 2 * c + z]
                )
            )
    for copy in loads:
        copy.start()
    barrier = pltpu.get_barrier_semaphore()
    xpeers = ring_peers(gx, nx, 2)
    ypeers = ring_peers(gy, ny, NEAR)
    inner = [peer for a, b, peer in ypeers if a == 0]
    outer = [peer for a, b, peer in ypeers if b == 0]
    for a, b, peer in xpeers:
        pl.semaphore_signal(barrier, inc=1, device_id={"gx": peer}, device_id_type=MESH)
    for peer in inner + outer:
        pl.semaphore_signal(barrier, inc=1, device_id={"gy": peer}, device_id_type=MESH)

    def share(axis, me, peers, buf, send, recv):
        copies = []
        for d, (a, b, peer) in enumerate(peers):
            copy = pltpu.make_async_remote_copy(
                src_ref=buf.at[me],
                dst_ref=buf.at[me],
                send_sem=send.at[d],
                recv_sem=recv.at[me],
                device_id={axis: peer},
                device_id_type=MESH,
            )
            copy.start()
            copies.append(copy)
        return copies

    def arrive(axis, peers, buf, send, recv):
        for d, (a, b, peer) in enumerate(peers):
            pltpu.make_async_remote_copy(
                src_ref=buf.at[peer],
                dst_ref=buf.at[peer],
                send_sem=send.at[d],
                recv_sem=recv.at[peer],
                device_id={axis: peer},
                device_id_type=MESH,
            ).wait_recv()

    for copy in loads[:2]:
        copy.wait()
    for z in range(2):
        eps[z] = 1.0 / (diffusion * visc[z])

    def eps_x(col, t):
        return eps[col, pl.ds(t, CH, stride=sx), :]

    def vel_x(c, col, t):
        return vel[c, col, pl.ds(t, CH, stride=sx), :]

    def eps_y(col, t):
        return eps_t[col, pl.ds(t, CH, stride=sy), :]

    def vel_y(c, col, t):
        return ut[c, col, pl.ds(t, CH, stride=sy), :]

    fundamental(eps_x, xphi, xpsi, xends, 2, sx)
    xwhole, xinv = chunk_states(xends, xstates, xcoef.at[gx], 2)
    pl.semaphore_wait(barrier, nx - 1 + len(inner) + len(outer))
    for peer in outer:
        pl.semaphore_signal(entered, inc=1, device_id={"gy": peer}, device_id_type=MESH)
    sent = share("gx", gx, xpeers, xcoef, xc_send, xc_recv)
    weights(eps_x, xphi, xpsi, xaw, xbw, xstates, xwhole, xinv, 2, sx)
    for copy in loads[2:]:
        copy.wait()
    for col in range(2):
        left, right = totals(vel_x, xaw, xbw, 2, sx, col)
        k = xinv[col : col + 1, :]
        for c in range(3):
            xtots[0, c, col] = left[c]
            xtots[1, c, col] = right[c]
            for lr, value in enumerate((left[c], right[c])):
                at = (c % 2) * 4 + lr * 2 + col
                row = k * jnp.sum(value, axis=0, keepdims=True)
                xsrc[gx, c // 2, at : at + 1, :] = row
    xsrc[gx, 1, 4:8, :] = jnp.zeros((4, LANES), jnp.float32)
    sent += share("gx", gx, xpeers, xsrc, xs_send, xs_recv)

    for z in range(2):
        for tile in range(2):
            eps_t[2 * z + tile] = eps[z, tile * LANES : (tile + 1) * LANES, :].T
    fundamental(eps_y, yphi, ypsi, yends, 4, sy)
    ywhole, yinv = chunk_states(yends, ystates, ycoef.at[gy], 4)
    interior(vel_x, xphi, xpsi, xaw, xbw, xtots, xpart, 2, sx)
    pl.semaphore_wait(entered, len(outer))
    sent += share("gy", gy, ypeers, ycoef, yc_send, yc_recv)
    weights(eps_y, yphi, ypsi, yaw, ybw, ystates, ywhole, yinv, 4, sy)
    arrive("gx", xpeers, xcoef, xc_send, xc_recv)
    green(xcoef, xnodes, xwts, gx, nx, 2)

    arrive("gx", xpeers, xsrc, xs_send, xs_recv)
    ends = []
    for side in range(2):
        tiles = []
        for k in range(2):
            acc = xwts[side, 0] * xsrc[0, k]
            for p in range(1, nx):
                acc = acc + xwts[side, p] * xsrc[p, k]
            tiles.append(acc + pltpu.roll(acc, CH - 2, 0))
        ends.append(tiles)
    for col in range(2):
        for c in range(3):
            at = (c % 2) * 4 + col
            s = row8(ends[0][c // 2][at : at + 1, :])
            r = row8(ends[1][c // 2][at : at + 1, :])
            for t in range(sx):
                vel[c, col, pl.ds(t, CH, stride=sx), :] = (
                    xpart[c, col, t] + xphi[col, t] * s + xpsi[col, t] * r
                )

    for col in range(4):
        z, tile = col // 2, col % 2
        for c in range(3):
            ut[c, col] = vel[c, z, tile * LANES : (tile + 1) * LANES, :].T
        left, right = totals(vel_y, yaw, ybw, 4, sy, col)
        k = yinv[col : col + 1, :]
        for c in range(3):
            ytots[0, c, col] = left[c]
            ytots[1, c, col] = right[c]
            for lr, value in enumerate((left[c], right[c])):
                at = lr * 4 + col
                ysrc[gy, c, at : at + 1, :] = k * jnp.sum(value, axis=0, keepdims=True)
    sent += share("gy", gy, ypeers, ysrc, ys_send, ys_recv)
    arrive("gy", ypeers, ycoef, yc_send, yc_recv)
    green(ycoef, ynodes, ywts, gy, ny, 4)
    interior(vel_y, yphi, ypsi, yaw, ybw, ytots, ypart, 4, sy)

    arrive("gy", ypeers, ysrc, ys_send, ys_recv)
    for side in range(2):
        for c in range(3):
            acc = ywts[side, 0] * ysrc[0, c]
            for p in range(1, ny):
                acc = acc + ywts[side, p] * ysrc[p, c]
            yends_out[side, c] = acc + pltpu.roll(acc, 4, 0)
    for copy in sent:
        copy.wait_send()


def finish(sy, ypart, yphi, ypsi, ends, out_hbm, turned, out, sem):
    stores = []
    for c in range(3):
        for z in range(2):
            for tile in range(2):
                col = 2 * z + tile
                s = row8(ends[0, c, col : col + 1, :])
                r = row8(ends[1, c, col : col + 1, :])
                for t in range(sy):
                    turned[c, col, pl.ds(t, CH, stride=sy), :] = (
                        ypart[c, col, t] + yphi[col, t] * s + ypsi[col, t] * r
                    )
                out[c, z, tile * LANES : (tile + 1) * LANES, :] = turned[c, col].T
            store = pltpu.make_async_copy(out.at[c, z], out_hbm.at[c, z], sem.at[2 * c + z])
            store.start()
            stores.append(store)
    for store in stores:
        store.wait()


def on_device(nx, ny, velocity, viscosity):
    lx, ly = velocity.shape[2], velocity.shape[3]
    sx, sy = lx // CH, ly // CH
    f32 = jnp.float32
    vm = lambda *shape: pltpu.VMEM(shape, f32)
    dma = lambda n: pltpu.SemaphoreType.DMA((n,))

    def phase(cols, steps, devices, rows, coefs, srcs):
        return [
            vm(cols, steps, CH, LANES),
            vm(cols, steps, CH, LANES),
            vm(4, cols, CH, LANES),
            vm(4, cols, CH, LANES),
            vm(2, 3, cols, CH, LANES),
            vm(2, devices + 1, rows, LANES),
            vm(2, devices, CH, LANES),
            vm(devices, coefs, LANES),
            vm(devices, srcs, CH, LANES),
        ]

    on_chip = pl.BlockSpec(memory_space=pltpu.VMEM)
    in_hbm = pl.BlockSpec(memory_space=pltpu.HBM)
    shape = lambda *dims: jax.ShapeDtypeStruct(dims, f32)
    xphase = phase(2, sx, nx, 2, 8, 2)
    kept = pl.pallas_call(
        functools.partial(kernel, nx, ny, sx, sy),
        out_shape=(
            shape(3, 4, sy, CH, LANES),
            shape(4, sy, CH, LANES),
            shape(4, sy, CH, LANES),
            shape(2, 3, CH, LANES),
        ),
        in_specs=[in_hbm] * 2,
        out_specs=(on_chip,) * 4,
        scratch_shapes=[
            vm(2, lx, ly),
            vm(3, 2, lx, ly),
            vm(2, lx, ly),
            vm(4, ly, LANES),
            vm(2, sx, CH, LANES),
            vm(2, sx, CH, LANES),
            *xphase[:5],
            vm(3, 2, sx, CH, LANES),
            *xphase[5:],
            *phase(4, sy, ny, 4, 16, 3),
            vm(3, 4, ly, LANES),
            dma(8),
            pltpu.SemaphoreType.REGULAR,
            dma(nx), dma(nx), dma(nx), dma(nx),
            dma(ny), dma(ny), dma(ny), dma(ny),
        ],
        compiler_params=pltpu.CompilerParams(
            collective_id=0, has_side_effects=True, vmem_limit_bytes=24 * 2**20
        ),
    )(
        pltpu.with_memory_space_constraint(viscosity, pltpu.HBM),
        pltpu.with_memory_space_constraint(velocity, pltpu.HBM),
    )
    return pl.pallas_call(
        functools.partial(finish, sy),
        out_shape=shape(*velocity.shape),
        in_specs=[on_chip] * 4,
        out_specs=in_hbm,
        scratch_shapes=[
            vm(3, 4, ly, LANES),
            vm(3, 2, lx, ly),
            dma(6),
        ],
        compiler_params=pltpu.CompilerParams(vmem_limit_bytes=16 * 2**20),
    )(*kept)


def solution(mesh):
    return jax.shard_map(
        functools.partial(on_device, mesh.shape["gx"], mesh.shape["gy"]),
        mesh=mesh,
        in_specs=(P(None, None, "gx", "gy"), P(None, "gx", "gy")),
        out_specs=P(None, None, "gx", "gy"),
        check_vma=False,
    )
```

```python
import functools

import jax
import jax.numpy as jnp
from jax import lax
from jax.experimental import pallas as pl
from jax.experimental.pallas import tpu as pltpu
from jax.sharding import PartitionSpec as P

diffusion = 10000.0
MESH = pl.DeviceIdType.MESH
CH = 8
LANES = 128


NEAR = 4


def ring_peers(me, devices, inner):
    outer = devices // inner
    mine_out, mine_in = me // inner, lax.rem(me, inner)
    far = lambda step, size: min(step, size - step) if size > 2 else 0
    steps = [(a, b) for a in range(outer) for b in range(inner) if a or b]
    steps.sort(key=lambda ab: -(far(ab[0], outer) + far(ab[1], inner)))
    return [
        (a, b, lax.rem(mine_out + a, outer) * inner + lax.rem(mine_in + b, inner))
        for a, b in steps
    ]


def row8(ref_or_value):
    return jnp.broadcast_to(ref_or_value, (CH, LANES))


def fundamental(eps, phi, psi, ends, cols, steps):
    one = jnp.ones((CH, LANES), jnp.float32)
    zero = jnp.zeros((CH, LANES), jnp.float32)
    state = [(one, zero, zero, one) for _ in range(cols)]
    for t in range(steps):
        for col in range(cols):
            a, da, b, db = state[col]
            phi[col, t] = a
            psi[col, t] = b
            e = eps[col, pl.ds(t, CH, stride=steps + 1), :]
            da = da + e * a
            db = db + e * b
            state[col] = (a + da, da, b + db, db)
    for col in range(cols):
        a, da, b, db = state[col]
        ends[0, col] = a
        ends[1, col] = b
        ends[2, col] = da
        ends[3, col] = db


def chunk_states(ends, states, coef, cols):
    one = jnp.ones((cols, LANES), jnp.float32)
    zero = jnp.zeros((cols, LANES), jnp.float32)
    f, df, m, v = one, zero, zero, one
    n, z = zero, one
    for q in range(CH):
        a, b, da, db = [ends[k, :, q, :] for k in range(4)]
        states[0, :, q, :] = m
        states[1, :, q, :] = v
        f, df = a * f + b * df, da * f + db * df
        m, v = a * m + b * v, da * m + db * v
        r = CH - 1 - q
        a, b, da, db = [ends[k, :, r, :] for k in range(4)]
        n, z = db * n + b * z, a * z + da * n
        states[2, :, r, :] = n
        states[3, :, r, :] = z
    coef[0 * cols : 1 * cols, :] = f
    coef[1 * cols : 2 * cols, :] = m
    coef[2 * cols : 3 * cols, :] = df
    coef[3 * cols : 4 * cols, :] = v
    return m, 1.0 / m


def weights(phi, psi, alpha, beta, states, inverse, cols, steps):
    pitch = steps + 1
    for col in range(cols):
        k = row8(inverse[col : col + 1, :])
        ms, vs, ns, zs = [states[j, col] * k for j in range(4)]
        for t in range(steps):
            a = phi[col, t]
            b = psi[col, t]
            alpha[col, pl.ds(t, CH, stride=pitch), :] = ns * a - zs * b
            beta[col, pl.ds(t, CH, stride=pitch), :] = ms * a + vs * b


def tile_rows(m, steps):
    per = steps // CH
    return pl.ds((m // per) * (steps + 1) + (m % per) * CH, CH)


def totals(load_f, eps, alpha, beta, steps, col, comps=range(3)):
    zero = jnp.zeros((CH, LANES), jnp.float32)
    left = [zero] * 3
    right = [zero] * 3
    for m in range(steps):
        rows = tile_rows(m, steps)
        e = eps[col, rows, :]
        a = alpha[col, rows, :]
        b = beta[col, rows, :]
        for c in comps:
            h = load_f(c, m) * e
            left[c] = left[c] + a * h
            right[c] = right[c] + b * h
    return left, right


def scan_up(x, places):
    for d in (1, 2, 4):
        x = x + jnp.where(places >= d, pltpu.roll(x, d, 0), 0.0)
    return x


def scan_down(x, places):
    for d in (1, 2, 4):
        x = x + jnp.where(places < CH - d, pltpu.roll(x, CH - d, 0), 0.0)
    return x


def interior(f, eps, alpha, beta, whole, part, cols, steps):
    pitch = steps + 1
    places = lax.broadcasted_iota(jnp.int32, (CH, LANES), 0)
    zero = jnp.zeros((CH, LANES), jnp.float32)
    for col in range(cols):
        w = row8(whole[col : col + 1, :])
        left = [zero] * 3
        right = [zero] * 3
        for t in range(steps):
            rows = pl.ds(t, CH, stride=pitch)
            we = eps[col, rows, :] * w
            aw, bw = alpha[col, rows, :] * we, beta[col, rows, :] * we
            for c in range(3):
                left[c] = left[c] + aw * f[c, col, rows, :]
                right[c] = right[c] + bw * f[c, col, rows, :]
        pre = [scan_up(right[c], places) - right[c] for c in range(3)]
        suf = [scan_down(left[c], places) for c in range(3)]
        for t in range(steps):
            rows = pl.ds(t, CH, stride=pitch)
            we = eps[col, rows, :] * w
            al, be = alpha[col, rows, :], beta[col, rows, :]
            for c in range(3):
                h = f[c, col, rows, :] * we
                pre[c] = pre[c] + be * h
                suf[c] = suf[c] - al * h
                part[c, col, rows, :] = al * pre[c] + be * suf[c]


def green(coef, nodes, wts, me, devices, rows):
    m = jnp.ones((rows, LANES), jnp.float32)
    v = m
    n = jnp.zeros((rows, LANES), jnp.float32)
    z = jnp.ones((rows, LANES), jnp.float32)
    ms, ns = [m], [n]
    nodes[0, 0] = m
    nodes[1, devices] = n
    for p in range(devices):
        a, b, da, db = [coef[p, k * rows : (k + 1) * rows, :] for k in range(4)]
        m, v = a * m + b * v, da * m + db * v
        ms.append(m)
        nodes[0, p + 1] = m
        r = devices - 1 - p
        a, b, da, db = [coef[r, k * rows : (k + 1) * rows, :] for k in range(4)]
        n, z = db * n + b * z, a * z + da * n
        ns.append(n)
        nodes[1, r] = n
    ns = ns[::-1]
    inverse = 1.0 / m
    for side in range(2):
        at = me + side
        mm = nodes[0, at] * inverse
        nn = nodes[1, at] * inverse
        g = [jnp.where(p <= at, ms[p] * nn, ns[p] * mm) for p in range(devices + 1)]
        for p in range(devices):
            pair = [g[p], g[p + 1]] * (CH // (2 * rows))
            wts[side, p] = jnp.concatenate(pair, axis=0)


def kernel(
    nx, ny, sx, sy,
    visc_hbm, vel_hbm, ypart, yalpha, ybeta, yends_out,
    visc, vel, eps, eps_t, velp, ut,
    xphi, xpsi, xalpha, xbeta, xends, xstates, xpart, xnodes, xwts, xcoef, xsrc,
    yphi, ypsi, yends, ystates, ynodes, ywts, ycoef, ysrc,
    in_sem, entered, sems,
):
    gx = lax.axis_index("gx")
    gy = lax.axis_index("gy")
    for z in range(2):
        pltpu.make_async_copy(visc_hbm.at[z], visc.at[z], in_sem.at[0]).start()
    for c in range(3):
        for z in range(2):
            pltpu.make_async_copy(vel_hbm.at[c, z], vel.at[c, z], in_sem.at[1]).start()
    barrier = pltpu.get_barrier_semaphore()
    xpeers = ring_peers(gx, nx, 2)
    ypeers = ring_peers(gy, ny, NEAR)
    inner = [peer for a, b, peer in ypeers if a == 0]
    outer = [peer for a, b, peer in ypeers if b == 0]
    for a, b, peer in xpeers:
        pl.semaphore_signal(barrier, inc=1, device_id={"gx": peer}, device_id_type=MESH)
    for peer in inner + outer:
        pl.semaphore_signal(barrier, inc=1, device_id={"gy": peer}, device_id_type=MESH)

    def share(axis, me, peers, buf, sem):
        for a, b, peer in peers:
            pltpu.make_async_remote_copy(
                src_ref=buf.at[me],
                dst_ref=buf.at[me],
                send_sem=sems.at[sem, 0],
                recv_sem=sems.at[sem, 1],
                device_id={axis: peer},
                device_id_type=MESH,
            ).start()

    def all_of(axis, peers, buf, sem):
        return pltpu.make_async_remote_copy(
            src_ref=buf.at[pl.ds(0, len(peers))],
            dst_ref=buf.at[pl.ds(0, len(peers))],
            send_sem=sems.at[sem, 0],
            recv_sem=sems.at[sem, 1],
            device_id={axis: peers[0][2]},
            device_id_type=MESH,
        )

    tx, ty = sx, sy
    pltpu.make_async_copy(visc_hbm, visc, in_sem.at[0]).wait()
    for z in range(2):
        for m in range(tx):
            eps[z, tile_rows(m, sx), :] = 1.0 / (diffusion * visc[z, m * CH : (m + 1) * CH, :])

    fundamental(eps, xphi, xpsi, xends, 2, sx)
    xwhole, xinv = chunk_states(xends, xstates, xcoef.at[gx], 2)
    pl.semaphore_wait(barrier, nx - 1 + len(inner) + len(outer))
    share("gx", gx, xpeers, xcoef, 0)
    weights(xphi, xpsi, xalpha, xbeta, xstates, xinv, 2, sx)
    pltpu.make_async_copy(vel_hbm, vel, in_sem.at[1]).wait()
    for col in range(2):
        left, right = totals(
            lambda c, m: vel[c, col, m * CH : (m + 1) * CH, :], eps, xalpha, xbeta, sx, col
        )
        for c in range(3):
            for lr, value in enumerate((left[c], right[c])):
                at = (c % 2) * 4 + lr * 2 + col
                xsrc[gx, c // 2, at : at + 1, :] = jnp.sum(value, axis=0, keepdims=True)
    xsrc[gx, 1, 4:8, :] = jnp.zeros((4, LANES), jnp.float32)
    share("gx", gx, xpeers, xsrc, 1)
    for peer in outer:
        pl.semaphore_signal(entered, inc=1, device_id={"gy": peer}, device_id_type=MESH)

    half = LANES // CH
    for z in range(2):
        for tile in range(2):
            turned = jnp.concatenate(
                [eps[z, tile_rows(tile * half + m, sx), :] for m in range(half)], axis=0
            ).T
            for m in range(ty):
                eps_t[2 * z + tile, tile_rows(m, sy), :] = turned[m * CH : (m + 1) * CH, :]
    fundamental(eps_t, yphi, ypsi, yends, 4, sy)
    ywhole, yinv = chunk_states(yends, ystates, ycoef.at[gy], 4)
    for c in range(3):
        for z in range(2):
            for m in range(tx):
                velp[c, z, tile_rows(m, sx), :] = vel[c, z, m * CH : (m + 1) * CH, :]
    pl.semaphore_wait(entered, len(outer))
    share("gy", gy, ypeers, ycoef, 2)
    interior(velp, eps, xalpha, xbeta, xwhole, xpart, 2, sx)
    weights(yphi, ypsi, yalpha, ybeta, ystates, yinv, 4, sy)
    all_of("gx", xpeers, xcoef, 0).wait_recv()
    green(xcoef, xnodes, xwts, gx, nx, 2)

    all_of("gx", xpeers, xsrc, 1).wait_recv()
    ends = []
    for side in range(2):
        tiles = []
        for k in range(2):
            acc = xwts[side, 0] * xsrc[0, k]
            for p in range(1, nx):
                acc = acc + xwts[side, p] * xsrc[p, k]
            tiles.append(acc + pltpu.roll(acc, CH - 2, 0))
        ends.append(tiles)
    for z in range(2):
        for tile in range(2):
            col = 2 * z + tile
            turned = []
            for c in range(3):
                at = (c % 2) * 4 + z
                s = row8(ends[0][c // 2][at : at + 1, :])
                r = row8(ends[1][c // 2][at : at + 1, :])
                block = []
                for m in range(half):
                    rows = tile_rows(tile * half + m, sx)
                    block.append(
                        xpart[c, z, rows, :] + xalpha[z, rows, :] * s + xbeta[z, rows, :] * r
                    )
                turned.append(jnp.concatenate(block, axis=0).T)
                for m in range(ty):
                    ut[c, col, tile_rows(m, sy), :] = turned[c][m * CH : (m + 1) * CH, :]
            left, right = totals(
                lambda c, m: turned[c][m * CH : (m + 1) * CH, :],
                eps_t, yalpha, ybeta, sy, col,
            )
            for c in range(3):
                for lr, value in enumerate((left[c], right[c])):
                    at = lr * 4 + col
                    ysrc[gy, c, at : at + 1, :] = jnp.sum(value, axis=0, keepdims=True)
    share("gy", gy, ypeers, ysrc, 3)
    all_of("gy", ypeers, ycoef, 2).wait_recv()
    green(ycoef, ynodes, ywts, gy, ny, 4)
    interior(ut, eps_t, yalpha, ybeta, ywhole, ypart, 4, sy)
    all_of("gx", xpeers, xcoef, 0).wait_send()
    all_of("gx", xpeers, xsrc, 1).wait_send()
    all_of("gy", ypeers, ycoef, 2).wait_send()

    all_of("gy", ypeers, ysrc, 3).wait_recv()
    for side in range(2):
        for c in range(3):
            acc = ywts[side, 0] * ysrc[0, c]
            for p in range(1, ny):
                acc = acc + ywts[side, p] * ysrc[p, c]
            yends_out[side, c] = acc + pltpu.roll(acc, 4, 0)
    all_of("gy", ypeers, ysrc, 3).wait_send()


def finish(sy, ypart, yalpha, ybeta, ends, out_hbm, out, sem):
    stores = []
    for c in range(3):
        for z in range(2):
            for tile in range(2):
                col = 2 * z + tile
                s = row8(ends[0, c, col : col + 1, :])
                r = row8(ends[1, c, col : col + 1, :])
                block = []
                for m in range(sy):
                    rows = tile_rows(m, sy)
                    block.append(
                        ypart[c, col, rows, :] + yalpha[col, rows, :] * s + ybeta[col, rows, :] * r
                    )
                out[c, z, tile * LANES : (tile + 1) * LANES, :] = jnp.concatenate(block, axis=0).T
            store = pltpu.make_async_copy(out.at[c, z], out_hbm.at[c, z], sem.at[2 * c + z])
            store.start()
            stores.append(store)
    for store in stores:
        store.wait()


def on_device(nx, ny, velocity, viscosity):
    lx, ly = velocity.shape[2], velocity.shape[3]
    sx, sy = lx // CH, ly // CH
    f32 = jnp.float32
    vm = lambda *shape: pltpu.VMEM(shape, f32)
    dma = lambda n: pltpu.SemaphoreType.DMA((n,))

    padx, pady = CH * (sx + 1), CH * (sy + 1)

    on_chip = pl.BlockSpec(memory_space=pltpu.VMEM)
    in_hbm = pl.BlockSpec(memory_space=pltpu.HBM)
    shape = lambda *dims: jax.ShapeDtypeStruct(dims, f32)
    kept = pl.pallas_call(
        functools.partial(kernel, nx, ny, sx, sy),
        out_shape=(
            shape(3, 4, pady, LANES),
            shape(4, pady, LANES),
            shape(4, pady, LANES),
            shape(2, 3, CH, LANES),
        ),
        in_specs=[in_hbm] * 2,
        out_specs=(on_chip,) * 4,
        scratch_shapes=[
            vm(2, lx, ly),
            vm(3, 2, lx, ly),
            vm(2, padx, LANES),
            vm(4, pady, LANES),
            vm(3, 2, padx, LANES),
            vm(3, 4, pady, LANES),
            vm(2, sx, CH, LANES),
            vm(2, sx, CH, LANES),
            vm(2, padx, LANES),
            vm(2, padx, LANES),
            vm(4, 2, CH, LANES),
            vm(4, 2, CH, LANES),
            vm(3, 2, padx, LANES),
            vm(2, nx + 1, 2, LANES),
            vm(2, nx, CH, LANES),
            vm(nx, 8, LANES),
            vm(nx, 2, CH, LANES),
            vm(4, sy, CH, LANES),
            vm(4, sy, CH, LANES),
            vm(4, 4, CH, LANES),
            vm(4, 4, CH, LANES),
            vm(2, ny + 1, 4, LANES),
            vm(2, ny, CH, LANES),
            vm(ny, 16, LANES),
            vm(ny, 3, CH, LANES),
            dma(2),
            pltpu.SemaphoreType.REGULAR,
            pltpu.SemaphoreType.DMA((4, 2)),
        ],
        compiler_params=pltpu.CompilerParams(
            collective_id=0, has_side_effects=True, vmem_limit_bytes=24 * 2**20
        ),
    )(
        pltpu.with_memory_space_constraint(viscosity, pltpu.HBM),
        pltpu.with_memory_space_constraint(velocity, pltpu.HBM),
    )
    return pl.pallas_call(
        functools.partial(finish, sy),
        out_shape=shape(*velocity.shape),
        in_specs=[on_chip] * 4,
        out_specs=in_hbm,
        scratch_shapes=[
            vm(3, 2, lx, ly),
            dma(6),
        ],
        compiler_params=pltpu.CompilerParams(vmem_limit_bytes=16 * 2**20),
    )(*kept)


def solution(mesh):
    return jax.shard_map(
        functools.partial(on_device, mesh.shape["gx"], mesh.shape["gy"]),
        mesh=mesh,
        in_specs=(P(None, None, "gx", "gy"), P(None, "gx", "gy")),
        out_specs=P(None, None, "gx", "gy"),
        check_vma=False,
    )
```
